128 devices in a mesh: tok: 8 (over z, core), exp: 16 (over y, x).
Axes of the slice: x: 4, y: 4, z: 4, core: 2. Of those that a mesh axis runs over, the one named last changes fastest.
Arguments:
- x_rows: bfloat16 [3072, 4096], P(('tok', 'exp')), may hold values from -6 to 6
- routes: int32 [3072, 8], P(('tok', 'exp')), may hold values from 0 to 31, all different within a row; in each aligned block of 24 rows (0 to 23, 24 to 47, ...) at most 7 rows name the same one
- base_weight: bfloat16 [32, 1536, 4096], P('exp', 'tok'), may hold values from -6 to 6
- keep_mask: int32 [32, 24, 64], P('exp', 'tok'), may hold values 0 or 1
- dual_start: float32 [32, 1536, 4096], P('exp', 'tok'), may hold values from -4 to 4
Outputs:
- weight: float32 [32, 1536, 4096], P('exp', 'tok')
- dual: float32 [32, 1536, 4096], P('exp', 'tok')
The draws below stay inside these ranges and needn't reach their ends.
Inputs may be any that keep to these rules, and one draw needn't show every extreme that they name: `routes`: each row names 8 different experts; among the rows of one device no expert is named more than 7 times, a bound that some block reaches; every expert is named by at least one token.
All inputs are finite; a program needn't handle non-finite values. No bound on the sum of `keep_mask` on one device may be relied on, other than what follows from the above.
Results may differ from the reference program's by a relative error of at most 0.0027.
Values may be sent and summed in bfloat16 or wider, within the bound.
A program may use at most 128 MiB of HBM per device.

```python
import math
import jax
import jax.numpy as jnp
import numpy as np
from jax import lax

D = 4096
HID = 1536
TOPK = 8
EXPERTS = 32
BLOCK = 64
ITERS = 2
ROWS_DEV = 24
TOKENS = 3072
MOST = 7
DEVICES = 128


def place_ends(entries, rng, smallest, high):
    dims = entries.shape
    spot = [jax.random.randint(jax.random.fold_in(rng, axis), (), 0, dims[axis]) for axis in range(len(dims))]
    entries = entries.at[tuple(spot)].set(smallest)
    longest = dims.index(max(dims))
    spot[longest] = (spot[longest] + 1) % dims[longest]
    return entries.at[tuple(spot)].set(high)


def steps_of(key, dims, pieces, least, high):
    def one(axis_at, shards_of):
        heights = jax.random.uniform(jax.random.fold_in(jax.random.fold_in(key, 6), axis_at), (shards_of,), jnp.float32, least / len(pieces), high / len(pieces))
        return jnp.repeat(jnp.exp(heights), dims[axis_at] // shards_of).reshape((-1,) + (1,) * (len(dims) - axis_at - 1))

    level = one(*pieces[0])
    for cut in pieces[1:]:
        level = level * one(*cut)
    return level


def routed_block(stream_key, own, number, rows, number_of, top, most, lean):
    ranking = jax.random.permutation(stream_key, number_of)
    heavy_load, usual = portions_of(number_of, rows * top, most, lean, True), portions_of(number_of, rows * top, most, lean, False)
    places = jnp.arange(number_of)

    def named(tallies, rotation):
        used = int((tallies > 0).sum())
        fixed = max(1, used // 4)
        shifted = fixed + (places - fixed + rotation * (used - fixed)) % max(1, number_of - fixed)
        return jnp.zeros((number_of,), jnp.int32).at[ranking[jnp.where(places < fixed, places, shifted)]].set(jnp.asarray(tallies, jnp.int32))

    tallies = jnp.where(number % 4 == 0, named(heavy_load, number // 4), named(usual, number - number // 4 - 1))
    mixed = jax.random.permutation(jax.random.fold_in(own, 3), number_of)
    source_of, taker = mixed[0:number_of // 2 * 2:2], mixed[1:number_of // 2 * 2:2]
    margin = jnp.minimum(tallies[source_of] - 1, most - tallies[taker]) // 2
    margin = jnp.where((source_of == ranking[0]) | (taker == ranking[0]) | (tallies[taker] == 0), 0, jnp.maximum(margin, 0))
    shifted = jax.random.randint(jax.random.fold_in(own, 4), (number_of // 2,), 0, 1 << 20) % (margin + 1)
    tallies = tallies.at[source_of].add(-shifted).at[taker].add(shifted)
    members = jnp.searchsorted(jnp.cumsum(tallies), jnp.arange(rows * top), side="right").astype(jnp.int32)
    table = members.reshape(top, rows).T
    table = table[jax.random.permutation(jax.random.fold_in(own, 1), rows)]
    rotation = jax.random.randint(jax.random.fold_in(own, 2), (rows, 1), 0, top)
    return jnp.take_along_axis(table, (jnp.arange(top)[None, :] + rotation) % top, axis=1)


def portions_of(amount, total, limit, skew, full):
    portions = [(1 << 20) // math.isqrt(standing ** skew) + 1 for standing in range(1, amount + 1)]
    largest = limit if full else min(limit, max(-(-total // amount), total * portions[0] // sum(portions)))
    least = 1 if total - largest >= amount - 1 else 0
    holding, surplus = [largest] + [least] * (amount - 1), total - largest - least * (amount - 1)
    while surplus > 0:
        movable = [i for i in range(1, amount) if holding[i] < largest] or [i for i in range(1, amount) if holding[i] < limit]
        whole, left = sum([portions[i] for i in movable]), surplus
        for i in movable:
            more = min(limit - holding[i], max(1, left * portions[i] // whole), surplus)
            holding[i] = holding[i] + more
            surplus = surplus - more
    return np.array(holding)


def bell_draw(own_key, extent, deviation, limit, cuts=(), kind=jnp.bfloat16):
    result = jax.random.normal(own_key, extent, jnp.float32) * deviation
    if len(cuts) > 0:
        result = steps_of(own_key, extent, cuts, -0.22, 0.18) * result
    return jnp.clip(result, min=-limit, max=limit).astype(kind)


def setup_inputs(seed: int = 0) -> dict:
    seeds = jax.random.split(jax.random.key(seed), 6)
    x_rows = bell_draw(seeds[0], (TOKENS, D), 1.0, 6.0, ((0, 128),))
    routes_keys = jax.random.split(jax.random.fold_in(seeds[1], 1), TOKENS // ROWS_DEV)
    routes_turns = jax.random.permutation(jax.random.fold_in(seeds[1], 3), TOKENS // ROWS_DEV)
    routes = jax.vmap(lambda own, number: routed_block(jax.random.fold_in(seeds[1], 2), own, number, ROWS_DEV, EXPERTS, TOPK, MOST, 1))(routes_keys, routes_turns).reshape((TOKENS, TOPK))
    base_weight = bell_draw(seeds[2], (EXPERTS, HID, D), 1.0, 6.0, ((0, 16), (1, 8)))
    keep_mask = place_ends((jax.random.randint(seeds[3], (EXPERTS, HID // BLOCK, D // BLOCK), 0, 2) < 1).astype(jnp.int32), jax.random.fold_in(seeds[3], 1), 0, 1)
    dual_start = bell_draw(seeds[4], (EXPERTS, HID, D), 0.5, 4.0, ((0, 16), (1, 8)), jnp.float32)
    return dict(x_rows=x_rows, routes=routes, base_weight=base_weight, keep_mask=keep_mask, dual_start=dual_start)


step_rate = 0.2
penalty = 1.0


def reference(x_rows, routes, base_weight, keep_mask, dual_start):
    labels = jnp.arange(EXPERTS, dtype=jnp.int32)
    hits = jnp.any(routes[:, :, None] == labels[None, None, :], axis=1)
    capacity = DEVICES * MOST

    def one_expert(items):
        hit, base, keep, dual = items
        count_int = jnp.sum(hit.astype(jnp.int32))
        count = count_int.astype(jnp.float32)
        index = jnp.nonzero(hit, size=capacity, fill_value=0)[0].astype(jnp.int32)
        live = (jnp.arange(capacity, dtype=jnp.int32) < count_int).astype(jnp.bfloat16)
        rows = x_rows[index] * live[:, None]
        mask = jnp.repeat(jnp.repeat(keep.astype(jnp.float32), BLOCK, 0), BLOCK, 1)
        base32 = base.astype(jnp.float32)
        weight = mask * base32
        zed = weight
        for step in range(ITERS):
            delta = (weight - base32).astype(jnp.bfloat16)
            resid = jnp.dot(rows, delta.T, preferred_element_type=jnp.float32).astype(jnp.bfloat16)
            grad = jnp.dot(resid.T, rows, preferred_element_type=jnp.float32) / count
            weight = weight - step_rate * (grad + penalty * (weight - zed + dual))
            zed = mask * (weight + dual)
            dual = dual + weight - zed
        return weight, dual

    weight, dual = lax.map(one_expert, (hits.T, base_weight, keep_mask, dual_start))
    return weight, dual
```

```python
import functools
import jax
import jax.numpy as jnp
from jax import lax
from jax.experimental import pallas as pl
from jax.experimental.pallas import tpu as pltpu

SLOTS = 896
HL = 192
D = 4096
CW = 512
NC = D // CW
BLOCK = 64
step_rate = 0.2
penalty = 1.0


def dot(a, b, ca, cb):
    return lax.dot_general(a, b, (((ca,), (cb,)), ((), ())), preferred_element_type=jnp.float32)


def tail_kernel(xc_hbm, r1_ref, base_hbm, dual_hbm, rm_ref, inv_ref, w_hbm, d_hbm,
                xc, base, dual, w1, r2, r2b, ow, od, sin, sout):
    def fetch(j):
        cols = pl.ds(j * CW, CW)
        return [
            pltpu.make_async_copy(xc_hbm.at[:, :, cols], xc.at[:, :, cols], sin.at[0, j]),
            pltpu.make_async_copy(base_hbm.at[:, :, cols], base.at[:, :, cols], sin.at[1, j]),
            pltpu.make_async_copy(dual_hbm.at[:, :, cols], dual.at[:, :, cols], sin.at[2, j]),
        ]
    for j in range(NC):
        for c in fetch(j):
            c.start()

    def mask_of(e, j):
        kb = lax.broadcasted_iota(jnp.int32, (BLOCK, CW), 0)
        cb = lax.broadcasted_iota(jnp.int32, (BLOCK, CW), 1) // BLOCK + j * (CW // BLOCK)
        sel = (kb == cb).astype(jnp.bfloat16)
        return dot(rm_ref[e], sel, 1, 0)

    def pass1(j, _):
        off = pl.multiple_of(j * CW, CW)
        cols = pl.ds(off, CW)
        for i, (h, v) in enumerate(((xc_hbm, xc), (base_hbm, base), (dual_hbm, dual))):
            pltpu.make_async_copy(h.at[:, :, cols], v.at[:, :, cols], sin.at[i, j]).wait()
        for e in range(2):
            x = xc[e, :, cols]
            g = dot(r1_ref[e], x, 1, 0) * inv_ref[e, 0:1, 0:1]
            m = mask_of(e, j)
            b = base[e, :, cols].astype(jnp.float32)
            w = m * b - step_rate * (g + penalty * dual[e, :, cols])
            w1[e, :, cols] = w
            dl = (w - b).astype(jnp.bfloat16)
            r = dot(dl, x, 1, 1)
            @pl.when(j == 0)
            def _():
                r2[e] = r
            @pl.when(j > 0)
            def _():
                r2[e] += r
        return 0
    lax.fori_loop(0, NC, pass1, 0)
    for e in range(2):
        r2b[e] = r2[e].astype(jnp.bfloat16)

    def outs(slot, off):
        cols = pl.ds(off, CW)
        return [
            pltpu.make_async_copy(ow.at[slot], w_hbm.at[:, :, cols], sout.at[0, slot]),
            pltpu.make_async_copy(od.at[slot], d_hbm.at[:, :, cols], sout.at[1, slot]),
        ]

    def pass2(j, _):
        off = pl.multiple_of(j * CW, CW)
        cols = pl.ds(off, CW)
        slot = j % 2
        @pl.when(j >= 2)
        def _():
            for c in outs(slot, off):
                c.wait()
        for e in range(2):
            g = dot(r2b[e], xc[e, :, cols], 1, 0) * inv_ref[e, 0:1, 0:1]
            m = mask_of(e, j)
            d0 = dual[e, :, cols]
            w = w1[e, :, cols]
            z = m * (w + d0)
            d1 = d0 + w - z
            w2 = w - step_rate * (g + penalty * (w - z + d1))
            z2 = m * (w2 + d1)
            ow[slot, e] = w2
            od[slot, e] = d1 + w2 - z2
        for c in outs(slot, off):
            c.start()
        return 0
    lax.fori_loop(0, NC, pass2, 0)
    for slot in range(2):
        for c in outs(slot, 0):
            c.wait()


def tail(xc, r1t, base, dual, rowmask, inv):
    any_ = pl.BlockSpec(memory_space=pl.ANY)
    vm = pl.BlockSpec(memory_space=pltpu.VMEM)
    out = jax.ShapeDtypeStruct((2, HL, D), jnp.float32)
    return pl.pallas_call(
        tail_kernel,
        out_shape=(out, out),
        in_specs=[any_, vm, any_, any_, vm, vm],
        out_specs=(any_, any_),
        scratch_shapes=[
            pltpu.VMEM((2, SLOTS, D), jnp.bfloat16),
            pltpu.VMEM((2, HL, D), jnp.bfloat16),
            pltpu.VMEM((2, HL, D), jnp.float32),
            pltpu.VMEM((2, HL, D), jnp.float32),
            pltpu.VMEM((2, HL, SLOTS), jnp.float32),
            pltpu.VMEM((2, HL, SLOTS), jnp.bfloat16),
            pltpu.VMEM((2, 2, HL, CW), jnp.float32),
            pltpu.VMEM((2, 2, HL, CW), jnp.float32),
            pltpu.SemaphoreType.DMA((3, NC)),
            pltpu.SemaphoreType.DMA((2, 2)),
        ],
        compiler_params=pltpu.CompilerParams(vmem_limit_bytes=60 * 1024 * 1024),
        name="tail",
    )(xc, r1t, base, dual, rowmask, inv)


def front(x_rows, routes, base_weight, keep_mask):
    rows = lax.all_gather(x_rows, ("tok", "exp"), axis=0, tiled=True)
    rts = lax.all_gather(routes, ("tok", "exp"), axis=0, tiled=True)
    e0 = 2 * lax.axis_index("exp")
    hits = jnp.stack([jnp.any(rts == e0 + i, axis=1) for i in range(2)]).astype(jnp.bfloat16)
    counts = jnp.sum(hits.astype(jnp.float32), axis=1)
    h = hits.reshape(2, 8, 384)
    up = (jnp.arange(384)[:, None] < jnp.arange(384)[None, :]).astype(jnp.bfloat16)
    rank = jnp.einsum("egr,rs->egs", h, up, preferred_element_type=jnp.float32)
    slot = jnp.where(h > 0, rank, -1.0)
    p = (slot[:, :, None, :] == jnp.arange(112, dtype=jnp.float32)[None, None, :, None]).astype(jnp.bfloat16)
    xc = jnp.einsum("egsr,grd->egsd", p, rows.reshape(8, 384, D), preferred_element_type=jnp.float32)
    xc = xc.astype(jnp.bfloat16).reshape(2, SLOTS, D)
    mask = jnp.repeat(jnp.repeat(keep_mask.astype(jnp.float32), BLOCK, 1), BLOCK, 2)
    delta = ((mask - 1.0) * base_weight.astype(jnp.float32)).astype(jnp.bfloat16)
    r1t = jnp.einsum("lcd,lnd->lcn", delta, xc, preferred_element_type=jnp.float32).astype(jnp.bfloat16)
    return xc, r1t, counts


def on_device(x_rows, routes, base_weight, keep_mask, dual_start):
    xc, r1t, counts = front(x_rows, routes, base_weight, keep_mask)
    rowmask = jnp.repeat(keep_mask, BLOCK, 1).astype(jnp.bfloat16)
    inv = jnp.broadcast_to((1.0 / counts)[:, None, None], (2, 8, 128))
    return tail(xc, r1t, base_weight, dual_start, rowmask, inv)


def solution(mesh):
    from jax.sharding import PartitionSpec as P
    return jax.shard_map(
        on_device,
        mesh=mesh,
        in_specs=(
            P(("tok", "exp"), None),
            P(("tok", "exp"), None),
            P("exp", "tok", None),
            P("exp", "tok", None),
            P("exp", "tok", None),
        ),
        out_specs=(P("exp", "tok", None), P("exp", "tok", None)),
        check_vma=False,
    )
```
